32 devices in a mesh: dp: 8 (over z, core), expert: 4 (over y, x).
Axes of the slice: x: 2, y: 2, z: 4, core: 2. Of those that a mesh axis runs over, the one named last changes fastest.
Arguments:
- images: bfloat16 [96, 197, 384], P(('dp', 'expert')), may hold values from -6 to 6
- teacher: bfloat16 [96, 197, 384], P(('dp', 'expert')), may hold values from -6 to 6
- out_grad: bfloat16 [96, 197, 384], P(('dp', 'expert')), may hold values from -6 to 6
- valid_mask: int32 [96, 197], P(('dp', 'expert')), may hold values from 0 to 1, as said below
- routes: int32 [96, 197, 2], P(('dp', 'expert')), may hold values from 0 to 7, all different within a row; in each aligned block of 591 rows (0 to 590, 591 to 1181, ..., all dimensions but the last counted through in order) at most 236 rows name the same one
- w_qkv: bfloat16 [384, 1152], P('dp'), may hold values from -0.3125 to 0.3125
- w_out: bfloat16 [384, 384], P('dp'), may hold values from -2 to 2
- gain_attn: bfloat16 [384], P('dp'), may hold values from 0.5 to 1.5
- gain_moe: bfloat16 [384], P('dp'), may hold values from 0.5 to 1.5
- router: bfloat16 [384, 8], P('dp'), may hold values from -0.21875 to 0.21875
- w_in: bfloat16 [8, 384, 1536], P('expert'), may hold values from -0.3125 to 0.3125
- w_back: bfloat16 [8, 1536, 384], P('expert'), may hold values from -0.21875 to 0.21875
Outputs:
- loss: float32 [], replicated
- output: bfloat16 [96, 197, 384], P(('dp', 'expert'))
- grad_images: bfloat16 [96, 197, 384], P(('dp', 'expert'))
- d_w_qkv: float32 [384, 1152], P('dp')
- d_w_out: float32 [384, 384], P('dp')
- d_gain_attn: float32 [384], P('dp')
- d_gain_moe: float32 [384], P('dp')
- d_router: float32 [384, 8], P('dp')
- d_w_in: float32 [8, 384, 1536], P('expert', 'dp')
- d_w_back: float32 [8, 1536, 384], P('expert', 'dp')
The draws below stay inside these ranges and needn't reach their ends.
Inputs may be any that keep to these rules, and one draw needn't show every extreme that they name: `routes`: the 2 experts of a token differ. Among the tokens of one device no expert is named more than 236 times. `valid_mask`: the first token of every image is valid.
All inputs are finite; a program needn't handle non-finite values.
Results may differ from the reference program's by a relative error of at most 0.013.
Values may be sent and summed in bfloat16 or wider, within the bound.
A program may use at most 192 MiB of HBM per device.

```python
import math
import jax
import jax.numpy as jnp
import numpy as np
from jax import lax

D = 384
HEADS = 6
HEAD_DIM = 64
FF = 1536
SEQ = 197
TOP = 2
EXPERTS = 8
IMAGES = 96
TOK_DEV = 591
TOKENS = 18912
CAP = 236
N_DP = 8
N_EXPERT = 4


def draw_valid_mask(key, part):
    rolls = jax.random.randint(key, (IMAGES, SEQ), 0, 4 * IMAGES)
    limit = IMAGES + 2 * jnp.arange(IMAGES, dtype=jnp.int32)[:, None]
    valid = (rolls < limit).astype(jnp.int32)
    first = (jnp.arange(SEQ, dtype=jnp.int32)[None, :] == 0).astype(jnp.int32)
    return jnp.maximum(valid, first)


def block_scale(stream_key, extent, pieces, least, top_value):
    loudness = 1.0
    for dim, parts in pieces:
        heights = jax.random.uniform(jax.random.fold_in(jax.random.fold_in(stream_key, 6), dim), (parts,), jnp.float32, least / len(pieces), top_value / len(pieces))
        loudness = loudness * jnp.repeat(jnp.exp(heights), extent[dim] // parts).reshape((-1,) + (1,) * (len(extent) - 1 - dim))
    return loudness


def routed_block(stream_key, own, number, rows, number_of, top, reach, lean):
    ranking = jax.random.permutation(stream_key, number_of)
    packed, common = load_shares(number_of, rows * top, reach, lean, True), load_shares(number_of, rows * top, reach, lean, False)
    places = jnp.arange(number_of)

    def named(tallies, turn):
        used = int((tallies > 0).sum())
        fixed = max(1, used // 4)
        shifted = fixed + (places - fixed + turn * (used - fixed)) % max(1, number_of - fixed)
        return jnp.zeros((number_of,), jnp.int32).at[ranking[jnp.where(places < fixed, places, shifted)]].set(jnp.asarray(tallies, jnp.int32))

    tallies = jnp.where(number % 4 == 0, named(packed, number // 4), named(common, number - number // 4 - 1))
    mixed = jax.random.permutation(jax.random.fold_in(own, 3), number_of)
    giver, taker = mixed[0:number_of // 2 * 2:2], mixed[1:number_of // 2 * 2:2]
    margin = jnp.minimum(tallies[giver] - 1, reach - tallies[taker]) // 2
    margin = jnp.where((giver == ranking[0]) | (taker == ranking[0]) | (tallies[taker] == 0), 0, jnp.maximum(margin, 0))
    shifted = jax.random.randint(jax.random.fold_in(own, 4), (number_of // 2,), 0, 1 << 20) % (margin + 1)
    tallies = tallies.at[giver].add(-shifted).at[taker].add(shifted)
    items = jnp.searchsorted(jnp.cumsum(tallies), jnp.arange(rows * top), side="right").astype(jnp.int32)
    table = items.reshape(top, rows).T
    table = table[jax.random.permutation(jax.random.fold_in(own, 1), rows)]
    turn = jax.random.randint(jax.random.fold_in(own, 2), (rows, 1), 0, top)
    return jnp.take_along_axis(table, (jnp.arange(top)[None, :] + turn) % top, axis=1)


def load_shares(amount, total, most, skew, full):
    weights = [(1 << 20) // math.isqrt(grade ** skew) + 1 for grade in range(1, amount + 1)]
    largest = most if full else min(most, max(-(-total // amount), total * weights[0] // sum(weights)))
    least = 1 if total - largest >= amount - 1 else 0
    given, rest = [largest] + [least] * (amount - 1), total - largest - least * (amount - 1)
    while rest > 0:
        candidates = [i for i in range(1, amount) if given[i] < largest] or [i for i in range(1, amount) if given[i] < most]
        whole, left = sum([weights[i] for i in candidates]), rest
        for i in candidates:
            more = min(most - given[i], max(1, left * weights[i] // whole), rest)
            given[i] = given[i] + more
            rest = rest - more
    return np.array(given)


def noise(rng, dims, deviation, reach, pieces=(), kind=jnp.bfloat16):
    factor_of = block_scale(rng, dims, pieces, -0.22, 0.18) if pieces else 1.0
    drawn = jax.random.normal(rng, dims, jnp.float32) * deviation * factor_of
    return jnp.minimum(jnp.maximum(drawn, -reach), reach).astype(kind)


def setup_inputs(seed: int = 0) -> dict:
    arg_keys = jax.random.split(jax.random.key(seed), 13)
    images = noise(arg_keys[0], (IMAGES, SEQ, D), 1.0, 6.0, ((0, 32),))
    teacher = noise(arg_keys[1], (IMAGES, SEQ, D), 1.0, 6.0, ((0, 32),))
    out_grad = noise(arg_keys[2], (IMAGES, SEQ, D), 1.0, 6.0, ((0, 32),))
    valid_mask = draw_valid_mask(jax.random.fold_in(arg_keys[12], 71), 0)
    routes_keys = jax.random.split(jax.random.fold_in(arg_keys[4], 1), IMAGES * SEQ // TOK_DEV)
    routes_turns = jax.random.permutation(jax.random.fold_in(arg_keys[4], 3), IMAGES * SEQ // TOK_DEV)
    routes = jax.vmap(lambda own, number: routed_block(jax.random.fold_in(arg_keys[4], 2), own, number, TOK_DEV, EXPERTS, TOP, CAP, 1))(routes_keys, routes_turns).reshape((IMAGES, SEQ, TOP))
    w_qkv = noise(arg_keys[5], (D, 3 * D), D ** -0.5, 0.3125, ((0, 8),))
    w_out = noise(arg_keys[6], (D, D), (max(1, D // 48)) ** -0.5, 2.0, ((0, 8),))
    gain_attn = jnp.clip(1.0 + 0.1 * jax.random.normal(arg_keys[7], (D,), jnp.float32), 0.5, 1.5).astype(jnp.bfloat16)
    gain_moe = jnp.clip(1.0 + 0.1 * jax.random.normal(arg_keys[8], (D,), jnp.float32), 0.5, 1.5).astype(jnp.bfloat16)
    router = noise(arg_keys[9], (D, EXPERTS), (2 * D) ** -0.5, 0.21875, ((0, 8),))
    w_in = noise(arg_keys[10], (EXPERTS, D, FF), D ** -0.5, 0.3125, ((0, 4),))
    w_back = noise(arg_keys[11], (EXPERTS, FF, D), (FF // 2) ** -0.5, 0.21875, ((0, 4),))
    return {"images": images, "teacher": teacher, "out_grad": out_grad, "valid_mask": valid_mask, "routes": routes, "w_qkv": w_qkv, "w_out": w_out, "gain_attn": gain_attn, "gain_moe": gain_moe, "router": router, "w_in": w_in, "w_back": w_back}


HIGHEST = lax.Precision.HIGHEST

@jax.custom_vjp
def low(v):
    return lax.optimization_barrier(v.astype(jnp.bfloat16)).astype(jnp.float32)

@jax.custom_vjp
def low_back(v):
    return v

def low_keep(v):
    return (low(v), None)

def low_pass(kept, grad):
    return (grad,)

def back_keep(v):
    return (v, None)

def back_low(kept, grad):
    return (low(grad),)
low.defvjp(low_keep, low_pass)
low_back.defvjp(back_keep, back_low)

def layer_norm(values, gain):
    middle = lax.optimization_barrier(jnp.mean(values, axis=-1, keepdims=True))
    center = values - middle
    variance = lax.optimization_barrier(jnp.mean(center * center, axis=-1, keepdims=True))
    return center * lax.rsqrt(variance + 1e-06) * gain

def attend(normed, w_qkv, w_out):
    group = normed.shape[0]
    projected = low_back(low(jnp.einsum('gsd,de->gse', normed, w_qkv, precision=HIGHEST)))
    projected = projected.reshape(group, SEQ, 3, HEADS, HEAD_DIM)
    query = projected[:, :, 0]
    keys = projected[:, :, 1]
    values = projected[:, :, 2]
    scores = low_back(jnp.einsum('gqhd,gkhd->ghqk', query, keys, precision=HIGHEST) * HEAD_DIM ** (-0.5))
    probs = low(jax.nn.softmax(scores, axis=-1))
    mixed = jnp.einsum('ghqk,gkhd->gqhd', probs, values, precision=HIGHEST)
    mixed = low_back(low(mixed)).reshape(group, SEQ, D)
    return low_back(jnp.einsum('gsd,de->gse', mixed, w_out, precision=HIGHEST))

def expert_apply(pack):
    rows_in, first, second = pack
    pre = low_back(jnp.dot(rows_in, first, precision=HIGHEST))
    activated = low(jax.nn.gelu(pre, approximate=False))
    return low_back(low(jnp.dot(activated, second, precision=HIGHEST)))

def reference(images, teacher, out_grad, valid_mask, routes, w_qkv, w_out, gain_attn, gain_moe, router, w_in, w_back):
    devices = N_DP * N_EXPERT
    flat = routes.reshape(devices, TOK_DEV * TOP).astype(jnp.int32)
    hits = (flat[:, :, None] == jnp.arange(EXPERTS, dtype=jnp.int32)[None, None, :]).astype(jnp.int32)
    order = lax.optimization_barrier(jnp.sum((jnp.cumsum(hits, axis=1) - 1) * hits, axis=2))
    place = jnp.arange(devices, dtype=jnp.int32)[:, None]
    slot = ((flat * devices + place) * CAP + order).reshape(-1).astype(jnp.int32)
    assigned = TOKENS * TOP
    owner = jnp.full((EXPERTS * devices * CAP,), assigned, jnp.int32).at[slot].set(jnp.arange(assigned, dtype=jnp.int32))
    source = jnp.where(owner < assigned, owner // TOP, TOKENS).astype(jnp.int32)
    route_rows = routes.reshape(TOKENS, TOP).astype(jnp.int32)
    mask_f = valid_mask.astype(jnp.float32)
    count = jnp.sum(mask_f)
    teach = teacher.astype(jnp.float32)

    def forward(inputs, wq, wo, gone, gtwo, wr, first, second):
        normed_one = low(layer_norm(inputs, gone))
        blocks = normed_one.reshape(IMAGES // 16, 16, SEQ, D)

        def block_attend(block):
            return attend(block, wq, wo)
        attn = lax.map(jax.checkpoint(block_attend), blocks).reshape(IMAGES, SEQ, D)
        hidden_one = inputs + attn
        normed_two = low(layer_norm(hidden_one, gtwo)).reshape(TOKENS, D)
        logits = low_back(jnp.dot(normed_two, wr, precision=HIGHEST))
        probs = jax.nn.softmax(logits, axis=-1)
        chosen = jnp.take_along_axis(probs, route_rows, axis=1)
        gates = chosen / lax.optimization_barrier(jnp.sum(chosen, axis=1, keepdims=True))
        padded = jnp.concatenate([normed_two, jnp.zeros((1, D), jnp.float32)], axis=0)
        sent = low_back(jnp.take(padded, source, axis=0)).reshape(EXPERTS, devices * CAP, D)
        made = lax.map(jax.checkpoint(expert_apply), (sent, first, second))
        picked = jnp.take(made.reshape(EXPERTS * devices * CAP, D), slot, axis=0).reshape(TOKENS, TOP, D)
        mixture = lax.optimization_barrier(jnp.sum(gates[:, :, None] * picked, axis=1))
        combined = hidden_one + mixture.reshape(IMAGES, SEQ, D)
        diff = combined - teach
        loss = jnp.sum(mask_f[:, :, None] * diff * diff) / (count * D)
        return (combined, loss)
    (combined, loss), pullback = jax.vjp(forward, images.astype(jnp.float32), w_qkv.astype(jnp.float32), w_out.astype(jnp.float32), gain_attn.astype(jnp.float32), gain_moe.astype(jnp.float32), router.astype(jnp.float32), w_in.astype(jnp.float32), w_back.astype(jnp.float32))
    grads = pullback((out_grad.astype(jnp.float32), jnp.asarray(TOKENS * D / 2, jnp.float32)))
    return (loss, combined.astype(jnp.bfloat16), grads[0].astype(jnp.bfloat16), grads[1], grads[2], grads[3], grads[4], grads[5], grads[6], grads[7])
```

```python
import functools
import math

import jax
import jax.numpy as jnp
from jax import lax
from jax.experimental import pallas as pl
from jax.experimental.pallas import tpu as pltpu
from jax.sharding import PartitionSpec as P

HEAD_DIM = 64
CORES = 2
LANES = 128
MESH = pl.DeviceIdType.MESH
F32 = jnp.float32
BF16 = jnp.bfloat16
ANY = pl.BlockSpec(memory_space=pl.ANY)
VMEM = pl.BlockSpec(memory_space=pltpu.VMEM)


def mm(a, b):
    return lax.dot_general(a, b, (((1,), (0,)), ((), ())), preferred_element_type=F32)


def mm_nt(a, b):
    return lax.dot_general(a, b, (((1,), (1,)), ((), ())), preferred_element_type=F32)


def mm_tn(a, b):
    return lax.dot_general(a, b, (((0,), (0,)), ((), ())), preferred_element_type=F32)


def iota(shape, dim):
    return lax.broadcasted_iota(jnp.int32, shape, dim)


def norm_stats(v):
    middle = jnp.mean(v, axis=-1, keepdims=True)
    center = v - middle
    variance = jnp.mean(center * center, axis=-1, keepdims=True)
    rstd = lax.rsqrt(variance + 1e-06)
    return center * rstd, rstd


def norm_back(grad, xhat, rstd, gain):
    inner = grad * gain
    first = jnp.mean(inner, axis=-1, keepdims=True)
    second = jnp.mean(inner * xhat, axis=-1, keepdims=True)
    return rstd * (inner - first - xhat * second)


def position():
    dp = lax.axis_index("dp")
    return dp // CORES, lax.rem(dp, CORES), lax.axis_index("expert")


def device(z, c, g):
    return {"dp": z * CORES + c, "expert": g}


def remote(src, dst, send_sem, recv_sem, where):
    return pltpu.make_async_remote_copy(
        src_ref=src,
        dst_ref=dst,
        send_sem=send_sem,
        recv_sem=recv_sem,
        device_id=where,
        device_id_type=MESH,
    )


def meet(peers):
    barrier = pltpu.get_barrier_semaphore()
    for peer in peers:
        pl.semaphore_signal(barrier, inc=1, device_id=peer, device_id_type=MESH)
    pl.semaphore_wait(barrier, len(peers))


def gather_kernel(n_z, shard, full, stage, send_z, recv_z, send_c, recv_c, local):
    z, c, g = position()
    own = z * CORES + c
    keep_in = pltpu.make_async_copy(shard, stage, local.at[0])
    keep_in.start()
    meet(
        [device(lax.rem(z + k, n_z), c, g) for k in range(1, n_z)]
        + [device(lax.rem(z + k, n_z), 1 - c, g) for k in range(n_z)]
    )

    def cross(src, index, slot):
        return remote(src, full.at[index], send_c.at[slot], recv_c.at[slot], device(z, 1 - c, g))

    cross(shard, own, 0).start()
    keep_in.wait()
    keep = pltpu.make_async_copy(stage, full.at[own], local.at[1])
    keep.start()
    for k in range(n_z - 1):
        for way in range(2):
            step = 1 - 2 * way
            origin = z - step * k
            index = lax.rem(origin + n_z, n_z) * CORES + c
            to = lax.rem(z + step + n_z, n_z)
            inside = (origin >= 0) & (origin < n_z) & (z + step >= 0) & (z + step < n_z)

            @pl.when(inside)
            def _():
                src = shard if k == 0 else full.at[index]
                remote(
                    src, full.at[index], send_z.at[way, k], recv_z.at[way, k], device(to, c, g)
                ).start()

        for way in range(2):
            step = 1 - 2 * way
            origin = z - step * (k + 1)
            index = lax.rem(origin + n_z, n_z) * CORES + c

            @pl.when((origin >= 0) & (origin < n_z))
            def _():
                remote(
                    shard, full.at[index], send_z.at[way, k], recv_z.at[way, k], device(z, 1 - c, g)
                ).wait_recv()
                cross(full.at[index], index, 1 + 2 * k + way).start()

    for k in range(n_z - 1):
        for way in range(2):
            step = 1 - 2 * way
            origin = z - step * k
            inside = (origin >= 0) & (origin < n_z) & (z + step >= 0) & (z + step < n_z)

            @pl.when(inside)
            def _():
                remote(
                    shard, full.at[own], send_z.at[way, k], recv_z.at[way, k], device(z, 1 - c, g)
                ).wait_send()

            origin = z - step * (k + 1)

            @pl.when((origin >= 0) & (origin < n_z))
            def _():
                cross(shard, own, 1 + 2 * k + way).wait()

    cross(shard, own, 0).wait()
    keep.wait()


def gather_weights(shard, n_dp):
    n_z = n_dp // CORES
    rows, cols = shard.shape
    return pl.pallas_call(
        functools.partial(gather_kernel, n_z),
        out_shape=jax.ShapeDtypeStruct((n_dp, rows, cols), shard.dtype),
        in_specs=[ANY],
        out_specs=ANY,
        scratch_shapes=[
            pltpu.VMEM((rows, cols), shard.dtype),
            pltpu.SemaphoreType.DMA((2, n_z - 1)),
            pltpu.SemaphoreType.DMA((2, n_z - 1)),
            pltpu.SemaphoreType.DMA((2 * n_z - 1,)),
            pltpu.SemaphoreType.DMA((2 * n_z - 1,)),
            pltpu.SemaphoreType.DMA((2,)),
        ],
        compiler_params=pltpu.CompilerParams(
            collective_id=0, has_side_effects=True, vmem_limit_bytes=4 << 20
        ),
        name="gather_weights",
    )(shard).reshape(n_dp * rows, cols)


def swap_kernel(parts, n_z, plane, sent, tile, arrived, tiles, stage, small, sends, recvs, tsend, trecv, local):
    z, c, g = position()
    me = g * CORES + c
    keep_in = pltpu.make_async_copy(sent.at[me], stage, local.at[0])
    keep_in.start()
    tile_in = pltpu.make_async_copy(tile, small, local.at[1])
    tile_in.start()
    others = [lax.rem(me + k, parts) for k in range(1, parts)]
    plane_peers = [device(z, lax.rem(e, CORES), e // CORES) for e in others]
    z_peers = [device(lax.rem(z + k, n_z), c, g) for k in range(1, n_z)]
    tile_peers = plane_peers if plane else z_peers
    tile_me = me if plane else z
    meet(plane_peers if plane else plane_peers + z_peers)
    copies = [
        remote(sent.at[e], arrived.at[me], sends.at[k], recvs.at[k], where)
        for k, (e, where) in enumerate(zip(others, plane_peers))
    ]
    copies += [
        remote(tile, tiles.at[tile_me], tsend.at[k], trecv.at[k], where)
        for k, where in enumerate(tile_peers)
    ]
    for copy in copies:
        copy.start()
    keep_in.wait()
    keep = pltpu.make_async_copy(stage, arrived.at[me], local.at[0])
    keep.start()
    tile_in.wait()
    tile_keep = pltpu.make_async_copy(small, tiles.at[tile_me], local.at[1])
    tile_keep.start()
    for copy in copies:
        copy.wait()
    keep.wait()
    tile_keep.wait()


def swap(sent, tile, n_z, plane, number):
    parts = sent.shape[0]
    count = parts if plane else n_z
    return pl.pallas_call(
        functools.partial(swap_kernel, parts, n_z, plane),
        out_shape=(
            jax.ShapeDtypeStruct(sent.shape, sent.dtype),
            jax.ShapeDtypeStruct((count, *tile.shape), tile.dtype),
        ),
        in_specs=[ANY, ANY],
        out_specs=(ANY, ANY),
        scratch_shapes=[
            pltpu.VMEM(sent.shape[1:], sent.dtype),
            pltpu.VMEM(tile.shape, tile.dtype),
            pltpu.SemaphoreType.DMA((parts - 1,)),
            pltpu.SemaphoreType.DMA((parts - 1,)),
            pltpu.SemaphoreType.DMA((count - 1,)),
            pltpu.SemaphoreType.DMA((count - 1,)),
            pltpu.SemaphoreType.DMA((2,)),
        ],
        compiler_params=pltpu.CompilerParams(
            collective_id=number, has_side_effects=True, vmem_limit_bytes=4 << 20
        ),
        name=f"swap_{number}",
    )(sent, tile)


def front_kernel(
    experts, slots, image, routes, routes_t, weights,
    proj_out, probs_out, mixed_out, hidden_out, meta_out, meta_t_out, sent_out, carry, carry_t,
):
    step = pl.program_id(0)
    width = image.shape[-1]
    seq = image.shape[1]
    heads = width // HEAD_DIM

    @pl.when(step == 0)
    def _():
        carry[...] = jnp.zeros_like(carry)
        carry_t[...] = jnp.zeros_like(carry_t)

    w_qkv = weights[:, : 3 * width]
    w_out = weights[:, 3 * width : 4 * width]
    misc = weights[:, 4 * width :]
    misc_t = misc.astype(F32).T
    gain_one = misc_t[experts : experts + 1]
    gain_two = misc_t[experts + 1 : experts + 2]
    x = image[0].astype(F32)
    xhat, _ = norm_stats(x)
    normed = (xhat * gain_one).astype(BF16)
    proj_out[0] = mm(normed, w_qkv).astype(BF16)
    scale = HEAD_DIM ** (-0.5)
    lower = iota((seq, LANES), 1) < HEAD_DIM
    for pair in range(heads // 2):
        at = pair * LANES
        query = proj_out[0, :, at : at + LANES]
        keys = proj_out[0, :, width + at : width + at + LANES]
        values = proj_out[0, :, 2 * width + at : 2 * width + at + LANES]
        outs = []
        for half in range(2):
            mask = lower if half == 0 else jnp.logical_not(lower)
            part = jnp.where(mask, query, jnp.zeros_like(query))
            scores = mm_nt(part, keys) * scale
            shifted = jnp.exp(scores - jnp.max(scores, axis=-1, keepdims=True))
            probs = shifted / jnp.sum(shifted, axis=-1, keepdims=True)
            probs_out[0, 2 * pair + half] = probs
            outs.append(mm(probs.astype(BF16), values))
        mixed_out[0, :, at : at + LANES] = jnp.where(lower, outs[0], outs[1]).astype(BF16)
    hidden = x + mm(mixed_out[0], w_out)
    hidden_out[0] = hidden
    hhat, _ = norm_stats(hidden)
    normed_two = (hhat * gain_two).astype(BF16)
    logits = mm(normed_two, misc)

    lane = iota((seq, LANES), 1)
    hit = [lane == routes[0, :, k : k + 1] for k in range(2)]
    own = [jnp.sum(jnp.where(h, logits, 0.0), axis=1, keepdims=True) for h in hit]
    gates = [1.0 / (1.0 + jnp.exp(own[1 - k] - own[k])) for k in range(2)]
    hits = jnp.where(hit[0] | hit[1], 1.0, 0.0)
    before = jnp.where(iota((seq, seq), 1) < iota((seq, seq), 0), 1.0, 0.0).astype(BF16)
    order = mm(before, hits.astype(BF16)) + carry[...]
    carry[...] += jnp.sum(hits, axis=0, keepdims=True)
    place = [
        routes[0, :, k : k + 1].astype(F32) * slots
        + jnp.sum(jnp.where(hit[k], order, 0.0), axis=1, keepdims=True)
        for k in range(2)
    ]
    meta = jnp.where(lane == 0, gates[0], jnp.where(lane == 1, gates[1], 0.0))
    meta_out[0] = jnp.where(lane == 2, place[0], jnp.where(lane == 3, place[1], meta))

    depth = carry_t.shape[0]
    row = iota((depth, seq), 0)
    hit_t = [row == routes_t[0, k : k + 1, :] for k in range(2)]
    hits_t = jnp.where(hit_t[0] | hit_t[1], 1.0, 0.0)
    after = jnp.where(iota((seq, seq), 0) < iota((seq, seq), 1), 1.0, 0.0).astype(BF16)
    order_t = mm(hits_t.astype(BF16), after) + carry_t[...]
    carry_t[...] += jnp.sum(hits_t, axis=1, keepdims=True)
    place_t = [
        routes_t[0, k : k + 1, :].astype(F32) * slots
        + jnp.sum(jnp.where(hit_t[k], order_t, 0.0), axis=0, keepdims=True)
        for k in range(2)
    ]
    for k in range(2):
        meta_t_out[0, k : k + 1, :] = place_t[k]

    def send(e, _):
        at = (iota((slots, seq), 0) + e * slots).astype(F32)
        pick = jnp.where((at == place_t[0]) | (at == place_t[1]), 1.0, 0.0).astype(BF16)
        rows = mm(pick, normed_two).astype(BF16)

        @pl.when(step == 0)
        def _():
            sent_out[e] = rows

        @pl.when(step > 0)
        def _():
            sent_out[e] = sent_out[e] + rows

        return 0

    lax.fori_loop(0, experts, send, 0)


def front(images, routes, weights, experts, slots):
    count, seq, width = images.shape
    heads = width // HEAD_DIM
    depth = -(-experts // 16) * 16
    routes_t = jnp.swapaxes(routes, 1, 2)

    def per_image(*shape):
        return pl.BlockSpec((1, *shape), lambda i: (i,) + (0,) * len(shape))

    def whole(*shape):
        return pl.BlockSpec(shape, lambda i: (0,) * len(shape))

    return pl.pallas_call(
        functools.partial(front_kernel, experts, slots),
        grid=(count,),
        out_shape=(
            jax.ShapeDtypeStruct((count, seq, 3 * width), BF16),
            jax.ShapeDtypeStruct((count, heads, seq, seq), F32),
            jax.ShapeDtypeStruct((count, seq, width), BF16),
            jax.ShapeDtypeStruct((count, seq, width), F32),
            jax.ShapeDtypeStruct((count, seq, LANES), F32),
            jax.ShapeDtypeStruct((count, 2, seq), F32),
            jax.ShapeDtypeStruct((experts, slots, width), BF16),
        ),
        in_specs=[
            per_image(seq, width),
            per_image(seq, 2),
            per_image(2, seq),
            whole(*weights.shape),
        ],
        out_specs=(
            per_image(seq, 3 * width),
            per_image(heads, seq, seq),
            per_image(seq, width),
            per_image(seq, width),
            per_image(seq, LANES),
            per_image(2, seq),
            whole(experts, slots, width),
        ),
        scratch_shapes=[pltpu.VMEM((1, LANES), F32), pltpu.VMEM((depth, 1), F32)],
        name="front",
    )(images, routes, routes_t, weights)


def gelu_pair(v):
    size = jnp.abs(v)
    t = 1.0 / (1.0 + (0.3275911 * math.sqrt(0.5)) * size)
    bell = jnp.exp(v * v * (-0.5))
    poly = t * (
        0.127414796
        + t * (-0.142248368 + t * (0.7107068705 + t * (-0.7265760135 + t * 0.5307027145)))
    )
    tail = poly * bell
    phi = jnp.where(v >= 0.0, 1.0 - tail, tail)
    return v * phi, phi + v * bell * (1.0 / math.sqrt(2.0 * math.pi))


def expert_kernel(core, x, w_in, w_back, tiles, act_out, slope_out, made_out, tile_out):
    hidden = w_in.shape[-1]
    block = 256
    rows = x[...]
    for n in range(hidden // block):
        cols = slice(n * block, (n + 1) * block)
        act, slope = gelu_pair(mm(rows, w_in[0, :, cols]))
        act_out[:, cols] = act.astype(BF16)
        slope_out[:, cols] = slope.astype(BF16)
    made_out[...] = mm(act_out[...], w_back[0]).astype(BF16)
    total = tiles[0]
    for k in range(1, tiles.shape[0]):
        total += tiles[k]
    tile_out[...] = total


def row_tile(rows):
    return rows // 4


def expert_forward(core, x, w_in, w_back, tiles):
    rows, width = x.shape
    hidden = w_in.shape[-1]
    tile = row_tile(rows)
    row_block = lambda cols: pl.BlockSpec((tile, cols), lambda i, c: (i, 0))
    return pl.pallas_call(
        expert_kernel,
        grid_spec=pltpu.PrefetchScalarGridSpec(
            num_scalar_prefetch=1,
            grid=(rows // tile,),
            in_specs=[
                row_block(width),
                pl.BlockSpec((1, width, hidden), lambda i, c: (c[0], 0, 0)),
                pl.BlockSpec((1, hidden, width), lambda i, c: (c[0], 0, 0)),
                pl.BlockSpec(tiles.shape, lambda i, c: (0, 0, 0)),
            ],
            out_specs=[
                row_block(hidden),
                row_block(hidden),
                row_block(width),
                pl.BlockSpec(tiles.shape[1:], lambda i, c: (0, 0)),
            ],
        ),
        out_shape=(
            jax.ShapeDtypeStruct((rows, hidden), BF16),
            jax.ShapeDtypeStruct((rows, hidden), BF16),
            jax.ShapeDtypeStruct((rows, width), BF16),
            jax.ShapeDtypeStruct(tiles.shape[1:], F32),
        ),
        name="expert_forward",
    )(core, x, w_in, w_back, tiles)


def middle_kernel(
    total_rows, experts, slots, back, hidden, meta, meta_t, teacher, out_grad, valid, tiles,
    output, grad_out, grad_logits, sent_out, square_out, count_out, squares, routes,
):
    step = pl.program_id(0)
    seq, width = hidden.shape[1:]
    count = jnp.sum(tiles[...], axis=0)[0:1, 0:1]
    places = [meta[0, :, 2 + k : 3 + k] for k in range(2)]
    gates = [meta[0, :, k : k + 1] for k in range(2)]
    all_slots = experts * slots
    chunk = chunk_of(all_slots)
    picked = [jnp.zeros((seq, width), F32) for _ in range(2)]
    for n in range(all_slots // chunk):
        at = (iota((seq, chunk), 1) + n * chunk).astype(F32)
        rows = back[n * chunk : (n + 1) * chunk]
        for k in range(2):
            pick = jnp.where(at == places[k], 1.0, 0.0).astype(BF16)
            picked[k] += mm(pick, rows)
    combined = hidden[0] + (gates[0] * picked[0] + gates[1] * picked[1])
    output[0] = combined.astype(BF16)
    diff = combined - teacher[0].astype(F32)
    masked = valid[0] * diff
    sq = jnp.sum(jnp.sum(masked * diff, axis=1, keepdims=True), axis=0, keepdims=True)

    @pl.when(step == 0)
    def _():
        squares[...] = jnp.zeros_like(squares)

    squares[...] += sq
    square_out[...] = squares[...]
    count_out[...] = jnp.zeros_like(count_out) + count
    grad = out_grad[0].astype(F32) + (total_rows / count) * masked
    grad_out[0] = grad
    grad_gates = [jnp.sum(p * grad, axis=1, keepdims=True) for p in picked]
    slope = gates[0] * gates[1] * (grad_gates[0] - grad_gates[1])
    lane = iota((seq, LANES), 1)
    hit = [lane == routes[0, :, k : k + 1] for k in range(2)]
    grad_logits[0] = jnp.where(hit[0], slope, jnp.where(hit[1], -slope, 0.0)).astype(BF16)
    weighted = [(g * grad).astype(BF16) for g in gates]
    places_t = [meta_t[0, k : k + 1, :] for k in range(2)]

    def send(e, _):
        at = (iota((slots, seq), 0) + e * slots).astype(F32)
        rows = jnp.zeros((slots, width), F32)
        for k in range(2):
            pick = jnp.where(at == places_t[k], 1.0, 0.0).astype(BF16)
            rows += mm(pick, weighted[k])
        rows = rows.astype(BF16)

        @pl.when(step == 0)
        def _():
            sent_out[e] = rows

        @pl.when(step > 0)
        def _():
            sent_out[e] = sent_out[e] + rows

        return 0

    lax.fori_loop(0, experts, send, 0)


def chunk_of(total):
    for chunk in (640, 512, 384, 256, 128):
        if total % chunk == 0:
            return chunk
    return total


def middle(total_rows, back, hidden, meta, meta_t, teacher, out_grad, valid, tiles, routes, experts, slots):
    count, seq, width = hidden.shape

    def per_image(*shape):
        return pl.BlockSpec((1, *shape), lambda i: (i,) + (0,) * len(shape))

    def whole(*shape):
        return pl.BlockSpec(shape, lambda i: (0,) * len(shape))

    def body(*refs):
        ins, route, rest = refs[:8], refs[8], refs[9:]
        middle_kernel(total_rows, experts, slots, *ins, *rest, route)

    return pl.pallas_call(
        body,
        grid=(count,),
        out_shape=(
            jax.ShapeDtypeStruct((count, seq, width), BF16),
            jax.ShapeDtypeStruct((count, seq, width), F32),
            jax.ShapeDtypeStruct((count, seq, LANES), BF16),
            jax.ShapeDtypeStruct((experts, slots, width), BF16),
            jax.ShapeDtypeStruct((8, LANES), F32),
            jax.ShapeDtypeStruct((8, LANES), F32),
        ),
        in_specs=[
            whole(*back.shape),
            per_image(seq, width),
            per_image(seq, LANES),
            per_image(2, seq),
            per_image(seq, width),
            per_image(seq, width),
            per_image(seq, 1),
            whole(*tiles.shape),
            per_image(seq, 2),
        ],
        out_specs=(
            per_image(seq, width),
            per_image(seq, width),
            per_image(seq, LANES),
            whole(experts, slots, width),
            whole(8, LANES),
            whole(8, LANES),
        ),
        scratch_shapes=[pltpu.VMEM((8, LANES), F32)],
        name="middle",
    )(back, hidden, meta, meta_t, teacher, out_grad, valid, tiles, routes)


def expert_back_kernel(core, grad, x, act, slope, w_in, w_back, grad_x, d_in, d_back, pre, sum_in, sum_back):
    step = pl.program_id(0)
    hidden = w_in.shape[-1]
    block = 256

    @pl.when(step == 0)
    def _():
        sum_in[...] = jnp.zeros_like(sum_in)
        sum_back[...] = jnp.zeros_like(sum_back)

    rows = grad[...]
    rows_t = rows.T
    x_t = x[...].T
    for n in range(hidden // block):
        cols = slice(n * block, (n + 1) * block)
        pre[:, cols] = (mm_nt(rows, w_back[0, cols, :]) * slope[:, cols].astype(F32)).astype(BF16)
        sum_back[:, cols] += mm(rows_t, act[:, cols])
        sum_in[:, cols] += mm(x_t, pre[:, cols])
    grad_x[...] = mm_nt(pre[...], w_in[0]).astype(BF16)

    @pl.when(step == pl.num_programs(0) - 1)
    def _():
        d_in[...] = sum_in[...].astype(BF16)
        for n in range(hidden // block):
            cols = slice(n * block, (n + 1) * block)
            d_back[cols, :] = sum_back[:, cols].T.astype(BF16)


def expert_backward(core, grad, x, act, slope, w_in, w_back):
    rows, width = x.shape
    hidden = w_in.shape[-1]
    tile = row_tile(rows)
    row_block = lambda cols: pl.BlockSpec((tile, cols), lambda i, c: (i, 0))
    return pl.pallas_call(
        expert_back_kernel,
        grid_spec=pltpu.PrefetchScalarGridSpec(
            num_scalar_prefetch=1,
            grid=(rows // tile,),
            in_specs=[
                row_block(width),
                row_block(width),
                row_block(hidden),
                row_block(hidden),
                pl.BlockSpec((1, width, hidden), lambda i, c: (c[0], 0, 0)),
                pl.BlockSpec((1, hidden, width), lambda i, c: (c[0], 0, 0)),
            ],
            out_specs=[
                row_block(width),
                pl.BlockSpec((width, hidden), lambda i, c: (0, 0)),
                pl.BlockSpec((hidden, width), lambda i, c: (0, 0)),
            ],
            scratch_shapes=[
                pltpu.VMEM((tile, hidden), BF16),
                pltpu.VMEM((width, hidden), F32),
                pltpu.VMEM((width, hidden), F32),
            ],
        ),
        out_shape=(
            jax.ShapeDtypeStruct((rows, width), BF16),
            jax.ShapeDtypeStruct((width, hidden), BF16),
            jax.ShapeDtypeStruct((hidden, width), BF16),
        ),
        name="expert_backward",
    )(core, grad, x, act, slope, w_in, w_back)


def piece_shape(n_g, rows, cols):
    row_parts = 2 if rows % 16 == 0 and n_g % 2 == 0 else 1
    col_parts = n_g // row_parts
    tiles = -(-cols // (LANES * col_parts))
    return row_parts, col_parts, rows // row_parts, tiles * LANES


def rear_kernel(
    experts, pieces, home, image, hidden, grad_out, grad_logits, meta, proj, probs, mixed, weights,
    grad_image, dense, sum_qkv, sum_out, sum_misc, grad_proj,
):
    step = pl.program_id(0)
    seq, width = image.shape[1:]
    heads = width // HEAD_DIM

    @pl.when(step == 0)
    def _():
        sum_qkv[...] = jnp.zeros_like(sum_qkv)
        sum_out[...] = jnp.zeros_like(sum_out)
        sum_misc[...] = jnp.zeros_like(sum_misc)

    w_qkv = weights[:, : 3 * width]
    w_out = weights[:, 3 * width : 4 * width]
    misc_t = weights[:, 4 * width :].astype(F32).T
    gain_one = misc_t[experts : experts + 1]
    gain_two = misc_t[experts + 1 : experts + 2]
    places = [meta[0, :, 2 + k : 3 + k] for k in range(2)]
    all_slots = home.shape[0]
    chunk = chunk_of(all_slots)
    logit_rows = grad_logits[0]
    grad_two = mm(logit_rows, misc_t.astype(BF16))
    for n in range(all_slots // chunk):
        at = (iota((seq, chunk), 1) + n * chunk).astype(F32)
        pick = jnp.where((at == places[0]) | (at == places[1]), 1.0, 0.0).astype(BF16)
        grad_two += mm(pick, home[n * chunk : (n + 1) * chunk])
    hhat, h_rstd = norm_stats(hidden[0])
    normed_two = (hhat * gain_two).astype(BF16)
    d_gain_two = jnp.sum(grad_two * hhat, axis=0, keepdims=True)
    grad_hidden = grad_out[0] + norm_back(grad_two, hhat, h_rstd, gain_two)
    grad_attn = grad_hidden.astype(BF16)
    sum_out[...] += mm_tn(mixed[0], grad_attn)
    grad_mixed = mm_nt(grad_attn, w_out).astype(BF16)
    d_router = mm_tn(logit_rows, normed_two)

    scale = HEAD_DIM ** (-0.5)
    lower = iota((seq, LANES), 1) < HEAD_DIM
    for pair in range(heads // 2):
        at = pair * LANES
        query = proj[0, :, at : at + LANES]
        keys = proj[0, :, width + at : width + at + LANES]
        values = proj[0, :, 2 * width + at : 2 * width + at + LANES]
        grad_pair = grad_mixed[:, at : at + LANES]
        got = []
        for half in range(2):
            mask = lower if half == 0 else jnp.logical_not(lower)
            part = jnp.where(mask, grad_pair, jnp.zeros_like(grad_pair))
            prob = probs[0, 2 * pair + half]
            grad_probs = mm_nt(part, values)
            inner = jnp.sum(grad_probs * prob, axis=-1, keepdims=True)
            grad_scores = (prob * (grad_probs - inner)).astype(BF16)
            got.append(
                (
                    mm(grad_scores, keys) * scale,
                    mm_tn(grad_scores, query) * scale,
                    mm_tn(prob.astype(BF16), grad_pair),
                )
            )
        for which in range(3):
            start = which * width + at
            grad_proj[:, start : start + LANES] = jnp.where(lower, got[0][which], got[1][which]).astype(BF16)
    xhat, x_rstd = norm_stats(image[0].astype(F32))
    normed_one = (xhat * gain_one).astype(BF16)
    sum_qkv[...] += mm_tn(normed_one, grad_proj[...])
    grad_one = mm_nt(grad_proj[...], w_qkv)
    d_gain_one = jnp.sum(grad_one * xhat, axis=0, keepdims=True)
    grad_image[0] = (grad_hidden + norm_back(grad_one, xhat, x_rstd, gain_one)).astype(BF16)
    row = iota((LANES, width), 0)
    sum_misc[...] += jnp.where(
        row == experts, d_gain_one, jnp.where(row == experts + 1, d_gain_two, d_router)
    )

    @pl.when(step == pl.num_programs(0) - 1)
    def _():
        n_z, blk, (row_parts, col_parts, rows, cols) = pieces
        misc = sum_misc[...].T
        for z in range(n_z):
            for c in range(CORES):
                for r in range(row_parts):
                    top = (z * CORES + c) * blk + r * rows
                    for tile in range(col_parts * cols // LANES):
                        left = tile * LANES
                        q, inside = left // cols, left % cols
                        if left < 3 * width:
                            value = sum_qkv[top : top + rows, left : left + LANES]
                        elif left < 4 * width:
                            value = sum_out[top : top + rows, left - 3 * width : left - 3 * width + LANES]
                        elif left == 4 * width:
                            value = misc[top : top + rows]
                        else:
                            value = jnp.zeros((rows, LANES), F32)
                        dense[c, r * col_parts + q, z, :, inside : inside + LANES] = value.astype(BF16)


def rear(home, images, hidden, grad_out, grad_logits, meta, proj, probs, mixed, weights, experts, n_z, n_g):
    count, seq, width = images.shape
    blk = width // (n_z * CORES)
    parts = piece_shape(n_g, blk, 4 * width + LANES)

    def per_image(*shape):
        return pl.BlockSpec((1, *shape), lambda i: (i,) + (0,) * len(shape))

    def whole(*shape):
        return pl.BlockSpec(shape, lambda i: (0,) * len(shape))

    dense = (CORES, n_g, n_z, parts[2], parts[3])
    return pl.pallas_call(
        functools.partial(rear_kernel, experts, (n_z, blk, parts)),
        grid=(count,),
        out_shape=(
            jax.ShapeDtypeStruct((count, seq, width), BF16),
            jax.ShapeDtypeStruct(dense, BF16),
        ),
        in_specs=[
            whole(*home.shape),
            per_image(seq, width),
            per_image(seq, width),
            per_image(seq, width),
            per_image(seq, LANES),
            per_image(seq, LANES),
            per_image(seq, 3 * width),
            per_image(*probs.shape[1:]),
            per_image(seq, width),
            whole(*weights.shape),
        ],
        out_specs=(per_image(seq, width), whole(*dense)),
        scratch_shapes=[
            pltpu.VMEM((width, 3 * width), F32),
            pltpu.VMEM((width, width), F32),
            pltpu.VMEM((LANES, width), F32),
            pltpu.VMEM((seq, 3 * width), BF16),
        ],
        name="rear",
    )(home, images, hidden, grad_out, grad_logits, meta, proj, probs, mixed, weights)


def reduce_kernel(
    n_z, n_g, width, parts, d_in, d_back, dense, square, count,
    out_in, out_back, out_qkv, out_out, out_misc, out_loss,
    own_in, own_back, got_in, got_back, give_in, give_back, take_in, take_back,
    own_dense, got_dense, sum_dense, got_sum, own_piece, all_pieces, sq_plane, sq_give, sq_line,
    s_exp, r_exp, s_core, r_core, s_a, r_a, s_b, r_b, s_c, r_c, s_q, r_q, s_l, r_l, local,
):
    z, c, g = position()
    me = g * CORES + c
    members = n_g * CORES
    row_parts, col_parts, rows, cols = parts
    others = [lax.rem(me + k, members) for k in range(1, members)]
    plane = [device(z, lax.rem(e, CORES), e // CORES) for e in others]
    line_z = [lax.rem(z + k, n_z) for k in range(1, n_z)]
    line = [device(other, c, g) for other in line_z]
    loads = [
        pltpu.make_async_copy(d_in.at[z], own_in, local.at[0]),
        pltpu.make_async_copy(d_back.at[z], own_back, local.at[1]),
        pltpu.make_async_copy(dense.at[c, g], own_dense, local.at[2]),
    ]
    for load in loads:
        load.start()
    meet(plane + line)
    step_a = [
        remote(
            dense.at[lax.rem(e, CORES), e // CORES], got_dense.at[k], s_a.at[k], r_a.at[k], where
        )
        for k, (e, where) in enumerate(zip(others, plane))
    ]
    step_q = [
        remote(square, sq_plane.at[k], s_q.at[k], r_q.at[k], where) for k, where in enumerate(plane)
    ]
    heavy = []
    for k, (other, where) in enumerate(zip(line_z, line)):
        heavy.append(remote(d_in.at[other], got_in.at[k], s_exp.at[0, k], r_exp.at[0, k], where))
        heavy.append(remote(d_back.at[other], got_back.at[k], s_exp.at[1, k], r_exp.at[1, k], where))
    for copy in step_a + step_q + heavy:
        copy.start()
    for load in loads:
        load.wait()
    for copy in step_a + step_q:
        copy.wait()
    for k in range(n_z):
        total = own_dense[k].astype(F32)
        for m in range(members - 1):
            total += got_dense[m, k].astype(F32)
        sum_dense[k] = total.astype(BF16)
    total = square[...]
    for m in range(members - 1):
        total += sq_plane[m]
    sq_give[...] = total
    step_b = [
        remote(sum_dense.at[other], got_sum.at[k], s_b.at[k], r_b.at[k], where)
        for k, (other, where) in enumerate(zip(line_z, line))
    ]
    step_l = [
        remote(sq_give, sq_line.at[k], s_l.at[k], r_l.at[k], where) for k, where in enumerate(line)
    ]
    for copy in step_b + step_l:
        copy.start()
    for copy in step_b + step_l:
        copy.wait()
    total = sum_dense[z].astype(F32)
    for k in range(n_z - 1):
        total += got_sum[k].astype(F32)
    own_piece[...] = total.astype(BF16)
    all_pieces[g] = own_piece[...]
    step_c = [
        remote(
            own_piece, all_pieces.at[g], s_c.at[k], r_c.at[k], device(z, c, lax.rem(g + k + 1, n_g))
        )
        for k in range(n_g - 1)
    ]
    for copy in step_c:
        copy.start()
    total = sq_give[...]
    for k in range(n_z - 1):
        total += sq_line[k]
    out_loss[...] = total / (count[...] * width)
    for copy in step_c:
        copy.wait()
    for r in range(row_parts):
        for tile in range(4 * width // LANES + 1):
            left = tile * LANES
            q, inside = left // cols, left % cols
            value = all_pieces[r * col_parts + q, :, inside : inside + LANES].astype(F32)
            span = slice(r * rows, (r + 1) * rows)
            if left < 3 * width:
                out_qkv[span, left : left + LANES] = value
            elif left < 4 * width:
                out_out[span, left - 3 * width : left - 3 * width + LANES] = value
            else:
                out_misc[span, :] = value

    for copy in heavy:
        copy.wait()
    for own, got, give, out in ((own_in, got_in, give_in, out_in), (own_back, got_back, give_back, out_back)):

        def total_of(half):
            total = own[half].astype(F32)
            for k in range(n_z - 1):
                total += got[k, half].astype(F32)
            return total

        give[...] = total_of(1 - c).astype(BF16)
        out[c] = total_of(c)
    partner = device(z, 1 - c, g)
    last = [
        remote(give_in, take_in, s_core.at[0], r_core.at[0], partner),
        remote(give_back, take_back, s_core.at[1], r_core.at[1], partner),
    ]
    for copy in last:
        copy.start()
    for copy in last:
        copy.wait()
    out_in[1 - c] = take_in[...].astype(F32)
    out_back[1 - c] = take_back[...].astype(F32)


def reduce_all(d_in, d_back, dense, square, count, n_z, n_g):
    width, hidden = d_in.shape
    blk_in = width // (n_z * CORES)
    blk_back = hidden // (n_z * CORES)
    parts = piece_shape(n_g, blk_in, 4 * width + LANES)
    members = n_g * CORES
    piece = dense.shape[-2:]
    dma = pltpu.SemaphoreType.DMA
    return pl.pallas_call(
        functools.partial(reduce_kernel, n_z, n_g, width, parts),
        out_shape=(
            jax.ShapeDtypeStruct((CORES, blk_in, hidden), F32),
            jax.ShapeDtypeStruct((CORES, blk_back, width), F32),
            jax.ShapeDtypeStruct((blk_in, 3 * width), F32),
            jax.ShapeDtypeStruct((blk_in, width), F32),
            jax.ShapeDtypeStruct((blk_in, LANES), F32),
            jax.ShapeDtypeStruct((8, LANES), F32),
        ),
        in_specs=[ANY, ANY, ANY, VMEM, VMEM],
        out_specs=(VMEM,) * 6,
        scratch_shapes=[
            pltpu.VMEM((CORES, blk_in, hidden), BF16),
            pltpu.VMEM((CORES, blk_back, width), BF16),
            pltpu.VMEM((n_z - 1, CORES, blk_in, hidden), BF16),
            pltpu.VMEM((n_z - 1, CORES, blk_back, width), BF16),
            pltpu.VMEM((blk_in, hidden), BF16),
            pltpu.VMEM((blk_back, width), BF16),
            pltpu.VMEM((blk_in, hidden), BF16),
            pltpu.VMEM((blk_back, width), BF16),
            pltpu.VMEM((n_z, *piece), BF16),
            pltpu.VMEM((members - 1, n_z, *piece), BF16),
            pltpu.VMEM((n_z, *piece), BF16),
            pltpu.VMEM((n_z - 1, *piece), BF16),
            pltpu.VMEM(piece, BF16),
            pltpu.VMEM((n_g, *piece), BF16),
            pltpu.VMEM((members - 1, 8, LANES), F32),
            pltpu.VMEM((8, LANES), F32),
            pltpu.VMEM((n_z - 1, 8, LANES), F32),
            dma((2, n_z - 1)),
            dma((2, n_z - 1)),
            dma((2,)),
            dma((2,)),
            dma((members - 1,)),
            dma((members - 1,)),
            dma((n_z - 1,)),
            dma((n_z - 1,)),
            dma((n_g - 1,)),
            dma((n_g - 1,)),
            dma((members - 1,)),
            dma((members - 1,)),
            dma((n_z - 1,)),
            dma((n_z - 1,)),
            dma((3,)),
        ],
        compiler_params=pltpu.CompilerParams(
            collective_id=5, has_side_effects=True, vmem_limit_bytes=32 << 20
        ),
        name="reduce_all",
    )(
        d_in.reshape(n_z, CORES, blk_in, hidden),
        d_back.reshape(n_z, CORES, blk_back, width),
        dense,
        square,
        count,
    )


def body(
    images, teacher, out_grad, valid_mask, routes, w_qkv, w_out, gain_attn, gain_moe, router, w_in, w_back
):
    img_count, seq, width = images.shape
    n_dp, n_g = lax.axis_size("dp"), lax.axis_size("expert")
    n_z = n_dp // CORES
    experts = n_g * w_in.shape[0]
    rows = img_count * seq
    capacity = max(2, rows * 16 // (experts * 5))
    slots = -(-capacity // 16) * 16
    total_rows = rows * n_dp * n_g
    core = lax.rem(lax.axis_index("dp"), CORES).astype(jnp.int32).reshape(1)
    valid = valid_mask.astype(F32)
    tile = jnp.zeros((8, LANES), F32) + jnp.sum(valid)
    shard = jnp.concatenate(
        [
            w_qkv,
            w_out,
            router,
            gain_attn[:, None],
            gain_moe[:, None],
            jnp.zeros((router.shape[0], LANES - experts - 2), BF16),
        ],
        axis=1,
    )
    weights = gather_weights(shard, n_dp)
    proj, probs, mixed, hidden, meta, meta_t, sent = front(images, routes, weights, experts, slots)
    arrived, tiles = swap(sent, tile, n_z, True, 1)
    x = arrived.reshape(experts * slots, width)
    act, slope, made, tile = expert_forward(core, x, w_in, w_back, tiles)
    back, tiles = swap(made.reshape(experts, slots, width), tile, n_z, False, 2)
    output, grad_out, grad_logits, sent, square, count = middle(
        total_rows, back.reshape(experts * slots, width), hidden, meta, meta_t, teacher, out_grad,
        valid[..., None], tiles, routes, experts, slots,
    )
    grads, _ = swap(sent, tile, n_z, True, 3)
    grad_x, d_in, d_back = expert_backward(
        core, grads.reshape(experts * slots, width), x, act, slope, w_in, w_back
    )
    home, _ = swap(grad_x.reshape(experts, slots, width), tile, n_z, True, 4)
    grad_images, dense = rear(
        home.reshape(experts * slots, width), images, hidden, grad_out, grad_logits, meta, proj, probs,
        mixed, weights, experts, n_z, n_g,
    )
    out_in, out_back, out_qkv, out_out, out_misc, loss = reduce_all(
        d_in, d_back, dense, square, count, n_z, n_g
    )
    return (
        loss[0, 0],
        output,
        grad_images,
        out_qkv,
        out_out,
        out_misc[:, experts],
        out_misc[:, experts + 1],
        out_misc[:, :experts],
        out_in,
        out_back,
    )


def solution(mesh):
    tokens = P(("dp", "expert"), None, None)
    in_specs = (
        tokens, tokens, tokens, P(("dp", "expert"), None), tokens,
        P("dp", None), P("dp", None), P("dp"), P("dp"), P("dp", None),
        P("expert", None, None), P("expert", None, None),
    )
    out_specs = (
        P(), tokens, tokens, P("dp", None), P("dp", None), P("dp"), P("dp"), P("dp", None),
        P("expert", "dp", None), P("expert", "dp", None),
    )
    return jax.shard_map(body, mesh=mesh, in_specs=in_specs, out_specs=out_specs, check_vma=False)
```

```python
import functools
import math

import jax
import jax.numpy as jnp
from jax import lax
from jax.experimental import pallas as pl
from jax.experimental.pallas import tpu as pltpu
from jax.sharding import PartitionSpec as P

HEAD_DIM = 64
CORES = 2
LANES = 128
MESH = pl.DeviceIdType.MESH
F32 = jnp.float32
BF16 = jnp.bfloat16
ANY = pl.BlockSpec(memory_space=pl.ANY)
VMEM = pl.BlockSpec(memory_space=pltpu.VMEM)


def mm(a, b):
    return lax.dot_general(a, b, (((1,), (0,)), ((), ())), preferred_element_type=F32)


def mm_nt(a, b):
    return lax.dot_general(a, b, (((1,), (1,)), ((), ())), preferred_element_type=F32)


def mm_tn(a, b):
    return lax.dot_general(a, b, (((0,), (0,)), ((), ())), preferred_element_type=F32)


def iota(shape, dim):
    return lax.broadcasted_iota(jnp.int32, shape, dim)


def norm_stats(v):
    middle = jnp.mean(v, axis=-1, keepdims=True)
    center = v - middle
    variance = jnp.mean(center * center, axis=-1, keepdims=True)
    rstd = lax.rsqrt(variance + 1e-06)
    return center * rstd, rstd


def norm_back(grad, xhat, rstd, gain):
    inner = grad * gain
    first = jnp.mean(inner, axis=-1, keepdims=True)
    second = jnp.mean(inner * xhat, axis=-1, keepdims=True)
    return rstd * (inner - first - xhat * second)


def position():
    dp = lax.axis_index("dp")
    return dp // CORES, lax.rem(dp, CORES), lax.axis_index("expert")


def device(z, c, g):
    return {"dp": z * CORES + c, "expert": g}


def remote(src, dst, send_sem, recv_sem, where):
    return pltpu.make_async_remote_copy(
        src_ref=src,
        dst_ref=dst,
        send_sem=send_sem,
        recv_sem=recv_sem,
        device_id=where,
        device_id_type=MESH,
    )


def meet(peers):
    barrier = pltpu.get_barrier_semaphore()
    for peer in peers:
        pl.semaphore_signal(barrier, inc=1, device_id=peer, device_id_type=MESH)
    pl.semaphore_wait(barrier, len(peers))


def gather_kernel(n_z, shard, full, stage, send_z, recv_z, send_c, recv_c, local):
    z, c, g = position()
    own = z * CORES + c
    keep_in = pltpu.make_async_copy(shard, stage, local.at[0])
    keep_in.start()
    meet(
        [device(lax.rem(z + k, n_z), c, g) for k in range(1, n_z)]
        + [device(lax.rem(z + k, n_z), 1 - c, g) for k in range(n_z)]
    )

    def cross(src, index, slot):
        return remote(src, full.at[index], send_c.at[slot], recv_c.at[slot], device(z, 1 - c, g))

    cross(shard, own, 0).start()
    keep_in.wait()
    keep = pltpu.make_async_copy(stage, full.at[own], local.at[1])
    keep.start()
    for k in range(n_z - 1):
        for way in range(2):
            step = 1 - 2 * way
            origin = z - step * k
            index = lax.rem(origin + n_z, n_z) * CORES + c
            to = lax.rem(z + step + n_z, n_z)
            inside = (origin >= 0) & (origin < n_z) & (z + step >= 0) & (z + step < n_z)

            @pl.when(inside)
            def _():
                src = shard if k == 0 else full.at[index]
                remote(
                    src, full.at[index], send_z.at[way, k], recv_z.at[way, k], device(to, c, g)
                ).start()

        for way in range(2):
            step = 1 - 2 * way
            origin = z - step * (k + 1)
            index = lax.rem(origin + n_z, n_z) * CORES + c

            @pl.when((origin >= 0) & (origin < n_z))
            def _():
                remote(
                    shard, full.at[index], send_z.at[way, k], recv_z.at[way, k], device(z, 1 - c, g)
                ).wait_recv()
                cross(full.at[index], index, 1 + 2 * k + way).start()

    for k in range(n_z - 1):
        for way in range(2):
            step = 1 - 2 * way
            origin = z - step * k
            inside = (origin >= 0) & (origin < n_z) & (z + step >= 0) & (z + step < n_z)

            @pl.when(inside)
            def _():
                remote(
                    shard, full.at[own], send_z.at[way, k], recv_z.at[way, k], device(z, 1 - c, g)
                ).wait_send()

            origin = z - step * (k + 1)

            @pl.when((origin >= 0) & (origin < n_z))
            def _():
                cross(shard, own, 1 + 2 * k + way).wait()

    cross(shard, own, 0).wait()
    keep.wait()


def gather_weights(shard, n_dp):
    n_z = n_dp // CORES
    rows, cols = shard.shape
    return pl.pallas_call(
        functools.partial(gather_kernel, n_z),
        out_shape=jax.ShapeDtypeStruct((n_dp, rows, cols), shard.dtype),
        in_specs=[ANY],
        out_specs=ANY,
        scratch_shapes=[
            pltpu.VMEM((rows, cols), shard.dtype),
            pltpu.SemaphoreType.DMA((2, n_z - 1)),
            pltpu.SemaphoreType.DMA((2, n_z - 1)),
            pltpu.SemaphoreType.DMA((2 * n_z - 1,)),
            pltpu.SemaphoreType.DMA((2 * n_z - 1,)),
            pltpu.SemaphoreType.DMA((2,)),
        ],
        compiler_params=pltpu.CompilerParams(
            collective_id=0, has_side_effects=True
        ),
        name="gather_weights",
    )(shard).reshape(n_dp * rows, cols)


def swap_kernel(parts, n_z, plane, sent, tile, arrived, tiles, stage, small, sends, recvs, tsend, trecv, local):
    z, c, g = position()
    me = g * CORES + c
    keep_in = pltpu.make_async_copy(sent.at[me], stage, local.at[0])
    keep_in.start()
    tile_in = pltpu.make_async_copy(tile, small, local.at[1])
    tile_in.start()
    others = [lax.rem(me + k, parts) for k in range(1, parts)]
    plane_peers = [device(z, lax.rem(e, CORES), e // CORES) for e in others]
    z_peers = [device(lax.rem(z + k, n_z), c, g) for k in range(1, n_z)]
    tile_peers = plane_peers if plane else z_peers
    tile_me = me if plane else z
    meet(plane_peers if plane else plane_peers + z_peers)
    copies = [
        remote(sent.at[e], arrived.at[me], sends.at[k], recvs.at[k], where)
        for k, (e, where) in enumerate(zip(others, plane_peers))
    ]
    copies += [
        remote(tile, tiles.at[tile_me], tsend.at[k], trecv.at[k], where)
        for k, where in enumerate(tile_peers)
    ]
    for copy in copies:
        copy.start()
    keep_in.wait()
    keep = pltpu.make_async_copy(stage, arrived.at[me], local.at[0])
    keep.start()
    tile_in.wait()
    tile_keep = pltpu.make_async_copy(small, tiles.at[tile_me], local.at[1])
    tile_keep.start()
    for copy in copies:
        copy.wait()
    keep.wait()
    tile_keep.wait()


def swap(sent, tile, n_z, plane, number):
    parts = sent.shape[0]
    count = parts if plane else n_z
    return pl.pallas_call(
        functools.partial(swap_kernel, parts, n_z, plane),
        out_shape=(
            jax.ShapeDtypeStruct(sent.shape, sent.dtype),
            jax.ShapeDtypeStruct((count, *tile.shape), tile.dtype),
        ),
        in_specs=[ANY, ANY],
        out_specs=(ANY, ANY),
        scratch_shapes=[
            pltpu.VMEM(sent.shape[1:], sent.dtype),
            pltpu.VMEM(tile.shape, tile.dtype),
            pltpu.SemaphoreType.DMA((parts - 1,)),
            pltpu.SemaphoreType.DMA((parts - 1,)),
            pltpu.SemaphoreType.DMA((count - 1,)),
            pltpu.SemaphoreType.DMA((count - 1,)),
            pltpu.SemaphoreType.DMA((2,)),
        ],
        compiler_params=pltpu.CompilerParams(
            collective_id=number, has_side_effects=True
        ),
        name=f"swap_{number}",
    )(sent, tile)


def front_kernel(
    experts, slots, image, routes, routes_t, weights,
    proj_out, probs_out, mixed_out, hidden_out, meta_out, meta_t_out, sent_out, carry, carry_t,
):
    step = pl.program_id(0)
    width = image.shape[-1]
    seq = image.shape[1]
    heads = width // HEAD_DIM

    @pl.when(step == 0)
    def _():
        carry[...] = jnp.zeros_like(carry)
        carry_t[...] = jnp.zeros_like(carry_t)

    w_qkv = weights[:, : 3 * width]
    w_out = weights[:, 3 * width : 4 * width]
    misc = weights[:, 4 * width :]
    misc_t = misc.astype(F32).T
    gain_one = misc_t[experts : experts + 1]
    gain_two = misc_t[experts + 1 : experts + 2]
    x = image[0].astype(F32)
    xhat, _ = norm_stats(x)
    normed = (xhat * gain_one).astype(BF16)
    proj_out[0] = mm(normed, w_qkv).astype(BF16)
    scale = HEAD_DIM ** (-0.5)
    lower = iota((seq, LANES), 1) < HEAD_DIM
    for pair in range(heads // 2):
        at = pair * LANES
        query = proj_out[0, :, at : at + LANES]
        keys = proj_out[0, :, width + at : width + at + LANES]
        values = proj_out[0, :, 2 * width + at : 2 * width + at + LANES]
        outs = []
        for half in range(2):
            mask = lower if half == 0 else jnp.logical_not(lower)
            part = jnp.where(mask, query, jnp.zeros_like(query))
            scores = mm_nt(part, keys) * scale
            shifted = jnp.exp(scores - jnp.max(scores, axis=-1, keepdims=True))
            probs = shifted / jnp.sum(shifted, axis=-1, keepdims=True)
            probs_out[0, 2 * pair + half] = probs
            outs.append(mm(probs.astype(BF16), values))
        mixed_out[0, :, at : at + LANES] = jnp.where(lower, outs[0], outs[1]).astype(BF16)
    hidden = x + mm(mixed_out[0], w_out)
    hidden_out[0] = hidden
    hhat, _ = norm_stats(hidden)
    normed_two = (hhat * gain_two).astype(BF16)
    logits = mm(normed_two, misc)

    lane = iota((seq, LANES), 1)
    hit = [lane == routes[0, :, k : k + 1] for k in range(2)]
    own = [jnp.sum(jnp.where(h, logits, 0.0), axis=1, keepdims=True) for h in hit]
    gates = [1.0 / (1.0 + jnp.exp(own[1 - k] - own[k])) for k in range(2)]
    hits = jnp.where(hit[0] | hit[1], 1.0, 0.0)
    before = jnp.where(iota((seq, seq), 1) < iota((seq, seq), 0), 1.0, 0.0).astype(BF16)
    order = mm(before, hits.astype(BF16)) + carry[...]
    carry[...] += jnp.sum(hits, axis=0, keepdims=True)
    place = [
        routes[0, :, k : k + 1].astype(F32) * slots
        + jnp.sum(jnp.where(hit[k], order, 0.0), axis=1, keepdims=True)
        for k in range(2)
    ]
    meta = jnp.where(lane == 0, gates[0], jnp.where(lane == 1, gates[1], 0.0))
    meta_out[0] = jnp.where(lane == 2, place[0], jnp.where(lane == 3, place[1], meta))

    depth = carry_t.shape[0]
    row = iota((depth, seq), 0)
    hit_t = [row == routes_t[0, k : k + 1, :] for k in range(2)]
    hits_t = jnp.where(hit_t[0] | hit_t[1], 1.0, 0.0)
    after = jnp.where(iota((seq, seq), 0) < iota((seq, seq), 1), 1.0, 0.0).astype(BF16)
    order_t = mm(hits_t.astype(BF16), after) + carry_t[...]
    carry_t[...] += jnp.sum(hits_t, axis=1, keepdims=True)
    place_t = [
        routes_t[0, k : k + 1, :].astype(F32) * slots
        + jnp.sum(jnp.where(hit_t[k], order_t, 0.0), axis=0, keepdims=True)
        for k in range(2)
    ]
    for k in range(2):
        meta_t_out[0, k : k + 1, :] = place_t[k]

    def send(e, _):
        at = (iota((slots, seq), 0) + e * slots).astype(F32)
        pick = jnp.where((at == place_t[0]) | (at == place_t[1]), 1.0, 0.0).astype(BF16)
        rows = mm(pick, normed_two).astype(BF16)

        @pl.when(step == 0)
        def _():
            sent_out[e] = rows

        @pl.when(step > 0)
        def _():
            sent_out[e] = sent_out[e] + rows

        return 0

    lax.fori_loop(0, experts, send, 0)


def front(images, routes, weights, experts, slots):
    count, seq, width = images.shape
    heads = width // HEAD_DIM
    depth = -(-experts // 16) * 16
    routes_t = jnp.swapaxes(routes, 1, 2)

    def per_image(*shape):
        return pl.BlockSpec((1, *shape), lambda i: (i,) + (0,) * len(shape))

    def whole(*shape):
        return pl.BlockSpec(shape, lambda i: (0,) * len(shape))

    return pl.pallas_call(
        functools.partial(front_kernel, experts, slots),
        grid=(count,),
        out_shape=(
            jax.ShapeDtypeStruct((count, seq, 3 * width), BF16),
            jax.ShapeDtypeStruct((count, heads, seq, seq), F32),
            jax.ShapeDtypeStruct((count, seq, width), BF16),
            jax.ShapeDtypeStruct((count, seq, width), F32),
            jax.ShapeDtypeStruct((count, seq, LANES), F32),
            jax.ShapeDtypeStruct((count, 2, seq), F32),
            jax.ShapeDtypeStruct((experts, slots, width), BF16),
        ),
        in_specs=[
            per_image(seq, width),
            per_image(seq, 2),
            per_image(2, seq),
            whole(*weights.shape),
        ],
        out_specs=(
            per_image(seq, 3 * width),
            per_image(heads, seq, seq),
            per_image(seq, width),
            per_image(seq, width),
            per_image(seq, LANES),
            per_image(2, seq),
            whole(experts, slots, width),
        ),
        scratch_shapes=[pltpu.VMEM((1, LANES), F32), pltpu.VMEM((depth, 1), F32)],
        name="front",
    )(images, routes, routes_t, weights)


def gelu_pair(v):
    size = jnp.abs(v)
    t = 1.0 / (1.0 + (0.3275911 * math.sqrt(0.5)) * size)
    bell = jnp.exp(v * v * (-0.5))
    poly = t * (
        0.127414796
        + t * (-0.142248368 + t * (0.7107068705 + t * (-0.7265760135 + t * 0.5307027145)))
    )
    tail = poly * bell
    phi = jnp.where(v >= 0.0, 1.0 - tail, tail)
    return v * phi, phi + v * bell * (1.0 / math.sqrt(2.0 * math.pi))


def expert_kernel(core, x, w_in, w_back, tiles, act_out, slope_out, made_out, tile_out):
    hidden = w_in.shape[-1]
    block = 256
    rows = x[...]
    for n in range(hidden // block):
        cols = slice(n * block, (n + 1) * block)
        act, slope = gelu_pair(mm(rows, w_in[0, :, cols]))
        act_out[:, cols] = act.astype(BF16)
        slope_out[:, cols] = slope.astype(BF16)
    made_out[...] = mm(act_out[...], w_back[0]).astype(BF16)
    total = tiles[0]
    for k in range(1, tiles.shape[0]):
        total += tiles[k]
    tile_out[...] = total


def row_tile(rows):
    return rows // 4


def expert_forward(core, x, w_in, w_back, tiles):
    rows, width = x.shape
    hidden = w_in.shape[-1]
    tile = row_tile(rows)
    row_block = lambda cols: pl.BlockSpec((tile, cols), lambda i, c: (i, 0))
    return pl.pallas_call(
        expert_kernel,
        grid_spec=pltpu.PrefetchScalarGridSpec(
            num_scalar_prefetch=1,
            grid=(rows // tile,),
            in_specs=[
                row_block(width),
                pl.BlockSpec((1, width, hidden), lambda i, c: (c[0], 0, 0)),
                pl.BlockSpec((1, hidden, width), lambda i, c: (c[0], 0, 0)),
                pl.BlockSpec(tiles.shape, lambda i, c: (0, 0, 0)),
            ],
            out_specs=[
                row_block(hidden),
                row_block(hidden),
                row_block(width),
                pl.BlockSpec(tiles.shape[1:], lambda i, c: (0, 0)),
            ],
        ),
        out_shape=(
            jax.ShapeDtypeStruct((rows, hidden), BF16),
            jax.ShapeDtypeStruct((rows, hidden), BF16),
            jax.ShapeDtypeStruct((rows, width), BF16),
            jax.ShapeDtypeStruct(tiles.shape[1:], F32),
        ),
        name="expert_forward",
    )(core, x, w_in, w_back, tiles)


def middle_kernel(
    total_rows, experts, slots, back, hidden, meta, meta_t, teacher, out_grad, valid, tiles,
    output, grad_out, grad_logits, sent_out, square_out, count_out, squares, routes,
):
    step = pl.program_id(0)
    seq, width = hidden.shape[1:]
    count = jnp.sum(tiles[...], axis=0)[0:1, 0:1]
    places = [meta[0, :, 2 + k : 3 + k] for k in range(2)]
    gates = [meta[0, :, k : k + 1] for k in range(2)]
    all_slots = experts * slots
    chunk = chunk_of(all_slots)
    picked = [jnp.zeros((seq, width), F32) for _ in range(2)]
    for n in range(all_slots // chunk):
        at = (iota((seq, chunk), 1) + n * chunk).astype(F32)
        rows = back[n * chunk : (n + 1) * chunk]
        for k in range(2):
            pick = jnp.where(at == places[k], 1.0, 0.0).astype(BF16)
            picked[k] += mm(pick, rows)
    combined = hidden[0] + (gates[0] * picked[0] + gates[1] * picked[1])
    output[0] = combined.astype(BF16)
    diff = combined - teacher[0].astype(F32)
    masked = valid[0] * diff
    sq = jnp.sum(jnp.sum(masked * diff, axis=1, keepdims=True), axis=0, keepdims=True)

    @pl.when(step == 0)
    def _():
        squares[...] = jnp.zeros_like(squares)

    squares[...] += sq
    square_out[...] = squares[...]
    count_out[...] = jnp.zeros_like(count_out) + count
    grad = out_grad[0].astype(F32) + (total_rows / count) * masked
    grad_out[0] = grad
    grad_gates = [jnp.sum(p * grad, axis=1, keepdims=True) for p in picked]
    slope = gates[0] * gates[1] * (grad_gates[0] - grad_gates[1])
    lane = iota((seq, LANES), 1)
    hit = [lane == routes[0, :, k : k + 1] for k in range(2)]
    grad_logits[0] = jnp.where(hit[0], slope, jnp.where(hit[1], -slope, 0.0)).astype(BF16)
    weighted = [(g * grad).astype(BF16) for g in gates]
    places_t = [meta_t[0, k : k + 1, :] for k in range(2)]

    def send(e, _):
        at = (iota((slots, seq), 0) + e * slots).astype(F32)
        rows = jnp.zeros((slots, width), F32)
        for k in range(2):
            pick = jnp.where(at == places_t[k], 1.0, 0.0).astype(BF16)
            rows += mm(pick, weighted[k])
        rows = rows.astype(BF16)

        @pl.when(step == 0)
        def _():
            sent_out[e] = rows

        @pl.when(step > 0)
        def _():
            sent_out[e] = sent_out[e] + rows

        return 0

    lax.fori_loop(0, experts, send, 0)


def chunk_of(total):
    for chunk in (640, 512, 384, 256, 128):
        if total % chunk == 0:
            return chunk
    return total


def middle(total_rows, back, hidden, meta, meta_t, teacher, out_grad, valid, tiles, routes, experts, slots):
    count, seq, width = hidden.shape

    def per_image(*shape):
        return pl.BlockSpec((1, *shape), lambda i: (i,) + (0,) * len(shape))

    def whole(*shape):
        return pl.BlockSpec(shape, lambda i: (0,) * len(shape))

    def body(*refs):
        ins, route, rest = refs[:8], refs[8], refs[9:]
        middle_kernel(total_rows, experts, slots, *ins, *rest, route)

    return pl.pallas_call(
        body,
        grid=(count,),
        out_shape=(
            jax.ShapeDtypeStruct((count, seq, width), BF16),
            jax.ShapeDtypeStruct((count, seq, width), F32),
            jax.ShapeDtypeStruct((count, seq, LANES), BF16),
            jax.ShapeDtypeStruct((experts, slots, width), BF16),
            jax.ShapeDtypeStruct((8, LANES), F32),
            jax.ShapeDtypeStruct((8, LANES), F32),
        ),
        in_specs=[
            whole(*back.shape),
            per_image(seq, width),
            per_image(seq, LANES),
            per_image(2, seq),
            per_image(seq, width),
            per_image(seq, width),
            per_image(seq, 1),
            whole(*tiles.shape),
            per_image(seq, 2),
        ],
        out_specs=(
            per_image(seq, width),
            per_image(seq, width),
            per_image(seq, LANES),
            whole(experts, slots, width),
            whole(8, LANES),
            whole(8, LANES),
        ),
        scratch_shapes=[pltpu.VMEM((8, LANES), F32)],
        name="middle",
    )(back, hidden, meta, meta_t, teacher, out_grad, valid, tiles, routes)


def expert_back_kernel(core, grad, x, act, slope, w_in, w_back, grad_x, d_in, d_back, pre, sum_in, sum_back):
    step = pl.program_id(0)
    hidden = w_in.shape[-1]
    block = 256

    @pl.when(step == 0)
    def _():
        sum_in[...] = jnp.zeros_like(sum_in)
        sum_back[...] = jnp.zeros_like(sum_back)

    rows = grad[...]
    rows_t = rows.T
    x_t = x[...].T
    for n in range(hidden // block):
        cols = slice(n * block, (n + 1) * block)
        pre[:, cols] = (mm_nt(rows, w_back[0, cols, :]) * slope[:, cols].astype(F32)).astype(BF16)
        sum_back[:, cols] += mm(rows_t, act[:, cols])
        sum_in[:, cols] += mm(x_t, pre[:, cols])
    grad_x[...] = mm_nt(pre[...], w_in[0]).astype(BF16)

    @pl.when(step == pl.num_programs(0) - 1)
    def _():
        d_in[...] = sum_in[...].astype(BF16)
        for n in range(hidden // block):
            cols = slice(n * block, (n + 1) * block)
            d_back[cols, :] = sum_back[:, cols].T.astype(BF16)


def expert_backward(core, grad, x, act, slope, w_in, w_back):
    rows, width = x.shape
    hidden = w_in.shape[-1]
    tile = row_tile(rows)
    row_block = lambda cols: pl.BlockSpec((tile, cols), lambda i, c: (i, 0))
    return pl.pallas_call(
        expert_back_kernel,
        grid_spec=pltpu.PrefetchScalarGridSpec(
            num_scalar_prefetch=1,
            grid=(rows // tile,),
            in_specs=[
                row_block(width),
                row_block(width),
                row_block(hidden),
                row_block(hidden),
                pl.BlockSpec((1, width, hidden), lambda i, c: (c[0], 0, 0)),
                pl.BlockSpec((1, hidden, width), lambda i, c: (c[0], 0, 0)),
            ],
            out_specs=[
                row_block(width),
                pl.BlockSpec((width, hidden), lambda i, c: (0, 0)),
                pl.BlockSpec((hidden, width), lambda i, c: (0, 0)),
            ],
            scratch_shapes=[
                pltpu.VMEM((tile, hidden), BF16),
                pltpu.VMEM((width, hidden), F32),
                pltpu.VMEM((width, hidden), F32),
            ],
        ),
        out_shape=(
            jax.ShapeDtypeStruct((rows, width), BF16),
            jax.ShapeDtypeStruct((width, hidden), BF16),
            jax.ShapeDtypeStruct((hidden, width), BF16),
        ),
        name="expert_backward",
    )(core, grad, x, act, slope, w_in, w_back)


def piece_shape(n_g, rows, cols):
    row_parts = 2 if rows % 16 == 0 and n_g % 2 == 0 else 1
    col_parts = n_g // row_parts
    tiles = -(-cols // (LANES * col_parts))
    return row_parts, col_parts, rows // row_parts, tiles * LANES


def rear_image(
    i, experts, home, image, hidden, grad_out, grad_logits, meta, proj, probs, mixed, weights, gains,
    router_t, grad_image, sum_qkv, sum_out, sum_misc, grad_proj,
):
    seq, width = image.shape[1:]
    heads = width // HEAD_DIM
    gain_one, gain_two = gains
    places = [meta[i, :, 2 + k : 3 + k] for k in range(2)]
    all_slots = home.shape[0]
    chunk = chunk_of(all_slots)
    logit_rows = grad_logits[i]
    grad_two = mm(logit_rows, router_t)
    for n in range(all_slots // chunk):
        at = (iota((seq, chunk), 1) + n * chunk).astype(F32)
        pick = jnp.where((at == places[0]) | (at == places[1]), 1.0, 0.0).astype(BF16)
        grad_two += mm(pick, home[n * chunk : (n + 1) * chunk])
    hhat, h_rstd = norm_stats(hidden[i])
    normed_two = (hhat * gain_two).astype(BF16)
    d_gain_two = jnp.sum(grad_two * hhat, axis=0, keepdims=True)
    grad_hidden = grad_out[i] + norm_back(grad_two, hhat, h_rstd, gain_two)
    grad_attn = grad_hidden.astype(BF16)
    sum_out[...] += mm_tn(mixed[i], grad_attn)
    grad_mixed = mm_nt(grad_attn, weights[:, 3 * width : 4 * width]).astype(BF16)
    d_router = mm_tn(logit_rows, normed_two)

    scale = HEAD_DIM ** (-0.5)
    lower = iota((seq, LANES), 1) < HEAD_DIM
    for pair in range(heads // 2):
        at = pair * LANES
        query = proj[i, :, at : at + LANES]
        keys = proj[i, :, width + at : width + at + LANES]
        values = proj[i, :, 2 * width + at : 2 * width + at + LANES]
        grad_pair = grad_mixed[:, at : at + LANES]
        got = []
        for half in range(2):
            mask = lower if half == 0 else jnp.logical_not(lower)
            part = jnp.where(mask, grad_pair, jnp.zeros_like(grad_pair))
            prob = probs[i, 2 * pair + half]
            grad_probs = mm_nt(part, values)
            inner = jnp.sum(grad_probs * prob, axis=-1, keepdims=True)
            grad_scores = (prob * (grad_probs - inner)).astype(BF16)
            got.append(
                (
                    mm(grad_scores, keys) * scale,
                    mm_tn(grad_scores, query) * scale,
                    mm_tn(prob.astype(BF16), grad_pair),
                )
            )
        for which in range(3):
            start = which * width + at
            grad_proj[:, start : start + LANES] = jnp.where(lower, got[0][which], got[1][which]).astype(BF16)
    xhat, x_rstd = norm_stats(image[i].astype(F32))
    normed_one = (xhat * gain_one).astype(BF16)
    sum_qkv[...] += mm_tn(normed_one, grad_proj[...])
    grad_one = mm_nt(grad_proj[...], weights[:, : 3 * width])
    d_gain_one = jnp.sum(grad_one * xhat, axis=0, keepdims=True)
    grad_image[i] = (grad_hidden + norm_back(grad_one, xhat, x_rstd, gain_one)).astype(BF16)
    row = iota((LANES, width), 0)
    sum_misc[...] += jnp.where(
        row == experts, d_gain_one, jnp.where(row == experts + 1, d_gain_two, d_router)
    )


def finish_kernel(
    n_z, n_g, experts, slots, parts,
    grad_x, image_h, hidden_h, grad_out_h, grad_logits_h, meta_h, proj_h, probs_h, mixed_h, weights_h,
    d_in, d_back, square, count,
    grad_image, out_in, out_back, out_qkv, out_out, out_misc, out_loss,
    home, image, hidden, grad_out, grad_logits, meta, proj, probs, mixed, weights,
    sum_qkv, sum_out, sum_misc, grad_proj, dense,
    own_in, own_back, got_in, got_back, give_in, give_back, take_in, take_back,
    got_dense, sum_dense, got_sum, own_piece, all_pieces, sq_plane, sq_give, sq_line,
    s_home, r_home, s_exp, r_exp, s_core, r_core, s_a, r_a, s_b, r_b, s_c, r_c, s_q, r_q, s_l, r_l, local,
):
    z, c, g = position()
    me = g * CORES + c
    members = n_g * CORES
    row_parts, col_parts, rows, cols = parts
    count_images, seq, width = image.shape
    others = [lax.rem(me + k, members) for k in range(1, members)]
    plane = [device(z, lax.rem(e, CORES), e // CORES) for e in others]
    line_z = [lax.rem(z + k, n_z) for k in range(1, n_z)]
    line = [device(other, c, g) for other in line_z]

    def slot_rows(e):
        return pl.ds(pl.multiple_of(e * slots, 16), slots)

    pairs = [
        (grad_x.at[me], home.at[slot_rows(me)]),
        (image_h, image), (hidden_h, hidden), (grad_out_h, grad_out), (grad_logits_h, grad_logits),
        (meta_h, meta), (proj_h, proj), (probs_h, probs), (mixed_h, mixed), (weights_h, weights),
        (d_in.at[z], own_in), (d_back.at[z], own_back),
    ]
    loads = [pltpu.make_async_copy(a, b, local.at[k]) for k, (a, b) in enumerate(pairs)]
    meet(plane + line)
    swaps = [
        remote(grad_x.at[e], home.at[slot_rows(me)], s_home.at[k], r_home.at[k], where)
        for k, (e, where) in enumerate(zip(others, plane))
    ]
    step_q = [
        remote(square, sq_plane.at[k], s_q.at[k], r_q.at[k], where) for k, where in enumerate(plane)
    ]
    heavy = []
    for k, (other, where) in enumerate(zip(line_z, line)):
        heavy.append(remote(d_in.at[other], got_in.at[k], s_exp.at[0, k], r_exp.at[0, k], where))
        heavy.append(remote(d_back.at[other], got_back.at[k], s_exp.at[1, k], r_exp.at[1, k], where))
    for copy in swaps + heavy + loads + step_q:
        copy.start()
    sum_qkv[...] = jnp.zeros_like(sum_qkv)
    sum_out[...] = jnp.zeros_like(sum_out)
    sum_misc[...] = jnp.zeros_like(sum_misc)
    for copy in loads + step_q:
        copy.wait()
    misc_t = weights[:, 4 * width :].astype(F32).T
    gains = (misc_t[experts : experts + 1], misc_t[experts + 1 : experts + 2])
    router_t = misc_t.astype(BF16)
    total = square[...]
    for m in range(members - 1):
        total += sq_plane[m]
    sq_give[...] = total
    for copy in swaps:
        copy.wait()

    def each(i, _):
        rear_image(
            i, experts, home, image, hidden, grad_out, grad_logits, meta, proj, probs, mixed, weights,
            gains, router_t, grad_image, sum_qkv, sum_out, sum_misc, grad_proj,
        )
        return 0

    lax.fori_loop(0, count_images, each, 0)

    blk = rows * row_parts
    misc = sum_misc[...].T
    for zz in range(n_z):
        for cc in range(CORES):
            for r in range(row_parts):
                top = (zz * CORES + cc) * blk + r * rows
                for tile in range(col_parts * cols // LANES):
                    left = tile * LANES
                    q, inside = left // cols, left % cols
                    if left < 3 * width:
                        value = sum_qkv[top : top + rows, left : left + LANES]
                    elif left < 4 * width:
                        value = sum_out[top : top + rows, left - 3 * width : left - 3 * width + LANES]
                    elif left == 4 * width:
                        value = misc[top : top + rows]
                    else:
                        value = jnp.zeros((rows, LANES), F32)
                    dense[cc, r * col_parts + q, zz, :, inside : inside + LANES] = value.astype(BF16)

    step_a = [
        remote(
            dense.at[lax.rem(e, CORES), e // CORES], got_dense.at[k], s_a.at[k], r_a.at[k], where
        )
        for k, (e, where) in enumerate(zip(others, plane))
    ]
    for copy in step_a:
        copy.start()
    for copy in step_a:
        copy.wait()
    for k in range(n_z):
        total = dense[c, g, k].astype(F32)
        for m in range(members - 1):
            total += got_dense[m, k].astype(F32)
        sum_dense[k] = total.astype(BF16)
    step_b = [
        remote(sum_dense.at[other], got_sum.at[k], s_b.at[k], r_b.at[k], where)
        for k, (other, where) in enumerate(zip(line_z, line))
    ]
    step_l = [
        remote(sq_give, sq_line.at[k], s_l.at[k], r_l.at[k], where) for k, where in enumerate(line)
    ]
    for copy in step_b + step_l:
        copy.start()

    for copy in heavy:
        copy.wait()
    for own, got, give, out in ((own_in, got_in, give_in, out_in), (own_back, got_back, give_back, out_back)):

        def total_of(half):
            total = own[half].astype(F32)
            for k in range(n_z - 1):
                total += got[k, half].astype(F32)
            return total

        give[...] = total_of(1 - c).astype(BF16)
        out[c] = total_of(c)
    partner = device(z, 1 - c, g)
    last = [
        remote(give_in, take_in, s_core.at[0], r_core.at[0], partner),
        remote(give_back, take_back, s_core.at[1], r_core.at[1], partner),
    ]
    for copy in last:
        copy.start()

    for copy in step_b + step_l:
        copy.wait()
    total = sum_dense[z].astype(F32)
    for k in range(n_z - 1):
        total += got_sum[k].astype(F32)
    own_piece[...] = total.astype(BF16)
    all_pieces[g] = own_piece[...]
    step_c = [
        remote(
            own_piece, all_pieces.at[g], s_c.at[k], r_c.at[k], device(z, c, lax.rem(g + k + 1, n_g))
        )
        for k in range(n_g - 1)
    ]
    for copy in step_c:
        copy.start()
    total = sq_give[...]
    for k in range(n_z - 1):
        total += sq_line[k]
    out_loss[...] = total / (count[...] * width)
    for copy in last:
        copy.wait()
    out_in[1 - c] = take_in[...].astype(F32)
    out_back[1 - c] = take_back[...].astype(F32)
    for copy in step_c:
        copy.wait()
    for r in range(row_parts):
        for tile in range(4 * width // LANES + 1):
            left = tile * LANES
            q, inside = left // cols, left % cols
            value = all_pieces[r * col_parts + q, :, inside : inside + LANES].astype(F32)
            span = slice(r * rows, (r + 1) * rows)
            if left < 3 * width:
                out_qkv[span, left : left + LANES] = value
            elif left < 4 * width:
                out_out[span, left - 3 * width : left - 3 * width + LANES] = value
            else:
                out_misc[span, :] = value


def finish(grad_x, saved, d_in, d_back, square, count, experts, n_z, n_g):
    images = saved[0]
    width, hidden = d_in.shape
    seq = images.shape[1]
    slots = grad_x.shape[1]
    blk_in = width // (n_z * CORES)
    blk_back = hidden // (n_z * CORES)
    parts = piece_shape(n_g, blk_in, 4 * width + LANES)
    members = n_g * CORES
    piece = parts[2:]
    dma = pltpu.SemaphoreType.DMA
    both = lambda n: [dma((n,)), dma((n,))]
    return pl.pallas_call(
        functools.partial(finish_kernel, n_z, n_g, experts, slots, parts),
        out_shape=(
            jax.ShapeDtypeStruct(images.shape, BF16),
            jax.ShapeDtypeStruct((CORES, blk_in, hidden), F32),
            jax.ShapeDtypeStruct((CORES, blk_back, width), F32),
            jax.ShapeDtypeStruct((blk_in, 3 * width), F32),
            jax.ShapeDtypeStruct((blk_in, width), F32),
            jax.ShapeDtypeStruct((blk_in, LANES), F32),
            jax.ShapeDtypeStruct((8, LANES), F32),
        ),
        in_specs=[ANY] * (3 + len(saved)) + [VMEM, VMEM],
        out_specs=(VMEM,) * 7,
        scratch_shapes=[
            pltpu.VMEM((experts * slots, width), BF16),
            *[pltpu.VMEM(v.shape, v.dtype) for v in saved],
            pltpu.VMEM((width, 3 * width), F32),
            pltpu.VMEM((width, width), F32),
            pltpu.VMEM((LANES, width), F32),
            pltpu.VMEM((seq, 3 * width), BF16),
            pltpu.VMEM((CORES, n_g, n_z, *piece), BF16),
            pltpu.VMEM((CORES, blk_in, hidden), BF16),
            pltpu.VMEM((CORES, blk_back, width), BF16),
            pltpu.VMEM((n_z - 1, CORES, blk_in, hidden), BF16),
            pltpu.VMEM((n_z - 1, CORES, blk_back, width), BF16),
            pltpu.VMEM((blk_in, hidden), BF16),
            pltpu.VMEM((blk_back, width), BF16),
            pltpu.VMEM((blk_in, hidden), BF16),
            pltpu.VMEM((blk_back, width), BF16),
            pltpu.VMEM((members - 1, n_z, *piece), BF16),
            pltpu.VMEM((n_z, *piece), BF16),
            pltpu.VMEM((n_z - 1, *piece), BF16),
            pltpu.VMEM(piece, BF16),
            pltpu.VMEM((n_g, *piece), BF16),
            pltpu.VMEM((members - 1, 8, LANES), F32),
            pltpu.VMEM((8, LANES), F32),
            pltpu.VMEM((n_z - 1, 8, LANES), F32),
            *both(members - 1),
            dma((2, n_z - 1)),
            dma((2, n_z - 1)),
            *both(2),
            *both(members - 1),
            *both(n_z - 1),
            *both(n_g - 1),
            *both(members - 1),
            *both(n_z - 1),
            dma((3 + len(saved),)),
        ],
        compiler_params=pltpu.CompilerParams(collective_id=5, has_side_effects=True),
        name="finish",
    )(
        grad_x,
        *saved,
        d_in.reshape(n_z, CORES, blk_in, hidden),
        d_back.reshape(n_z, CORES, blk_back, width),
        square,
        count,
    )


def body(
    images, teacher, out_grad, valid_mask, routes, w_qkv, w_out, gain_attn, gain_moe, router, w_in, w_back
):
    img_count, seq, width = images.shape
    n_dp, n_g = lax.axis_size("dp"), lax.axis_size("expert")
    n_z = n_dp // CORES
    experts = n_g * w_in.shape[0]
    rows = img_count * seq
    capacity = max(2, rows * 16 // (experts * 5))
    slots = -(-capacity // 16) * 16
    total_rows = rows * n_dp * n_g
    core = lax.rem(lax.axis_index("dp"), CORES).astype(jnp.int32).reshape(1)
    valid = valid_mask.astype(F32)
    tile = jnp.zeros((8, LANES), F32) + jnp.sum(valid)
    shard = jnp.concatenate(
        [
            w_qkv,
            w_out,
            router,
            gain_attn[:, None],
            gain_moe[:, None],
            jnp.zeros((router.shape[0], LANES - experts - 2), BF16),
        ],
        axis=1,
    )
    weights = gather_weights(shard, n_dp)
    proj, probs, mixed, hidden, meta, meta_t, sent = front(images, routes, weights, experts, slots)
    arrived, tiles = swap(sent, tile, n_z, True, 1)
    x = arrived.reshape(experts * slots, width)
    act, slope, made, tile = expert_forward(core, x, w_in, w_back, tiles)
    back, tiles = swap(made.reshape(experts, slots, width), tile, n_z, False, 2)
    output, grad_out, grad_logits, sent, square, count = middle(
        total_rows, back.reshape(experts * slots, width), hidden, meta, meta_t, teacher, out_grad,
        valid[..., None], tiles, routes, experts, slots,
    )
    grads, _ = swap(sent, tile, n_z, True, 3)
    grad_x, d_in, d_back = expert_backward(
        core, grads.reshape(experts * slots, width), x, act, slope, w_in, w_back
    )
    grad_images, out_in, out_back, out_qkv, out_out, out_misc, loss = finish(
        grad_x.reshape(experts, slots, width),
        (images, hidden, grad_out, grad_logits, meta, proj, probs, mixed, weights),
        d_in, d_back, square, count, experts, n_z, n_g,
    )
    return (
        loss[0, 0],
        output,
        grad_images,
        out_qkv,
        out_out,
        out_misc[:, experts],
        out_misc[:, experts + 1],
        out_misc[:, :experts],
        out_in,
        out_back,
    )


def solution(mesh):
    tokens = P(("dp", "expert"), None, None)
    in_specs = (
        tokens, tokens, tokens, P(("dp", "expert"), None), tokens,
        P("dp", None), P("dp", None), P("dp"), P("dp"), P("dp", None),
        P("expert", None, None), P("expert", None, None),
    )
    out_specs = (
        P(), tokens, tokens, P("dp", None), P("dp", None), P("dp"), P("dp"), P("dp", None),
        P("expert", "dp", None), P("expert", "dp", None),
    )
    return jax.shard_map(body, mesh=mesh, in_specs=in_specs, out_specs=out_specs, check_vma=False)
```
